32 devices in a mesh: gx: 4 (over y, x), gy: 8 (over z, core).
Axes of the slice: x: 2, y: 2, z: 4, core: 2. Of those that a mesh axis runs over, the one named last changes fastest.
Arguments:
- displacement: float32 [3, 16, 256, 1024], P(None, None, 'gx', 'gy'), may hold values from -1.2 to 1.2
- velocity: float32 [3, 16, 256, 1024], P(None, None, 'gx', 'gy'), may hold values from -6 to 6
- shear: float32 [15, 256, 1024], P(None, 'gx', 'gy'), may hold values from 0.3 to 3
- normals: float32 [3, 256, 1024], P(None, 'gx', 'gy'), may hold values from -1 to 1
- gap_zero: float32 [256, 1024], P('gx', 'gy'), may hold values from -0.3 to 0.1
- mortar: bfloat16 [256, 8, 128, 128], P('gx', 'gy'), may hold values from -1 to 1
- owner: int32 [256, 8], P('gx', 'gy'), may hold values from 0 to 7, as said below
- blocks: int32 [256, 8], P('gx', 'gy'), may hold values from 0 to 63
- live_rows: int32 [4, 8], P('gx', 'gy'), may hold values from 16 to 64, as said below
Outputs:
- new_displacement: float32 [3, 16, 256, 1024], P(None, None, 'gx', 'gy')
- new_velocity: float32 [3, 16, 256, 1024], P(None, None, 'gx', 'gy')
The draws below stay inside these ranges and needn't reach their ends.
Inputs may be any that keep to these rules, and one draw needn't show every extreme that they name: owner[r, j] = (j + 4 + e) mod 1024 / 128 with e one of -1, 0, 1. Slave blocks of rows 0 to live_rows - 1 of a tile are in contact; some tile has all 64 in every draw.
All inputs are finite; a program needn't handle non-finite values.
Results may differ from the reference program's by a relative error of at most 0.0003.
Values sent between devices are 32-bit elements; how exact they have to be, the bound alone decides.
A program may use at most 64 MiB of HBM per device.

```python
import math
import jax
import jax.numpy as jnp
from jax import lax

DEPTH = 16
ROWS_DEV = 64
BLOCK = 128
STEPS = 2
ROWS = 256
COLS = 1024
N_GX = 4
N_GY = 8


def draw_normals(key, part):
    first, second = jax.random.split(jax.random.fold_in(key, 11))
    tilt_rows = 0.5 * jax.random.normal(first, (ROWS, COLS), jnp.float32)
    tilt_cols = 0.5 * jax.random.normal(second, (ROWS, COLS), jnp.float32)
    length = jnp.sqrt(1.0 + tilt_rows * tilt_rows + tilt_cols * tilt_cols)
    return jnp.stack([jnp.ones((ROWS, COLS), jnp.float32), tilt_rows, tilt_cols], 0) / length


def draw_mortar(key, part):
    inner = jax.random.fold_in(key, 23)
    noise = jnp.clip(jax.random.normal(inner, (ROWS, N_GY, BLOCK, BLOCK), jnp.float32), -4.0, 4.0)
    coupling = 0.5 * jnp.eye(BLOCK, dtype=jnp.float32) + noise * (0.5 / jnp.sqrt(1.0 * BLOCK))
    return coupling.astype(jnp.bfloat16)


def draw_owner(key, part):
    column = jnp.arange(N_GY, dtype=jnp.int32)
    halfway = N_GY // 2
    offset = jax.random.randint(jax.random.fold_in(key, 37), (ROWS, N_GY), -1, 2, jnp.int32)
    return jnp.mod(column[None, :] + halfway + offset, N_GY).astype(jnp.int32)


def draw_live_rows(key, part):
    first, second = jax.random.split(jax.random.fold_in(key, 53))
    counts = jax.random.randint(first, (N_GX * N_GY,), ROWS_DEV // 4, ROWS_DEV + 1, jnp.int32)
    chosen = jax.random.randint(second, (), 0, N_GX * N_GY, jnp.int32)
    return counts.at[chosen].set(ROWS_DEV).reshape(N_GX, N_GY)


def touch_ends(result, own_key, least, top_value):
    longest = result.shape.index(max(result.shape))
    spots = []
    for shift in (0, 1):
        where = [jax.random.randint(jax.random.fold_in(own_key, axis), (), 0, length) for axis, length in enumerate(result.shape)]
        where[longest] = (where[longest] + shift) % result.shape[longest]
        spots.append(tuple(where))
    return result.at[spots[0]].set(least).at[spots[1]].set(top_value)


def steps_of(own_key, shape, shards, least, largest):
    gain = 1.0
    for position, parts in shards:
        draws = jax.random.uniform(jax.random.fold_in(jax.random.fold_in(own_key, 6), position), (parts,), jnp.float32, least / len(shards), largest / len(shards))
        gain = gain * jnp.repeat(jnp.exp(draws), shape[position] // parts).reshape((-1,) + (1,) * (len(shape) - 1 - position))
    return gain


def scatter_about(stream_key, shape, deviation, most, shards=(), held_as=jnp.bfloat16):
    entries = jax.random.normal(stream_key, shape, jnp.float32) * deviation
    if len(shards) > 0:
        entries = steps_of(stream_key, shape, shards, -0.22, 0.18) * entries
    return jnp.clip(entries, min=-most, max=most).astype(held_as)


def setup_inputs(seed: int = 0) -> dict:
    keys = jax.random.split(jax.random.key(seed), 10)
    displacement = scatter_about(keys[0], (3, DEPTH, ROWS, COLS), 0.2, 1.2, ((2, 4), (3, 8)), jnp.float32)
    velocity = scatter_about(keys[1], (3, DEPTH, ROWS, COLS), 1.0, 6.0, ((2, 4), (3, 8)), jnp.float32)
    shear = jnp.clip(jnp.exp(math.log(3.0) - 2.3025851 * jax.random.uniform(keys[2], (DEPTH - 1, ROWS, COLS), jnp.float32) ** steps_of(keys[2], (DEPTH - 1, ROWS, COLS), ((1, 4), (2, 8)), -0.2, 0.2)), 0.3, 3.0)
    normals = draw_normals(jax.random.fold_in(keys[9], 71), 0)
    gap_zero = jnp.clip(-0.3 + 0.4 * jax.random.uniform(keys[4], (ROWS, COLS), jnp.float32) ** steps_of(keys[4], (ROWS, COLS), ((0, 4), (1, 8)), -0.2, 0.2), -0.3, 0.1)
    mortar = draw_mortar(jax.random.fold_in(keys[9], 71), 0)
    owner = draw_owner(jax.random.fold_in(keys[9], 71), 0)
    blocks = touch_ends(jax.random.randint(keys[7], (ROWS, N_GY), 0, ROWS_DEV), jax.random.fold_in(keys[7], 1), 0, ROWS_DEV - 1).astype(jnp.int32)
    live_rows = draw_live_rows(jax.random.fold_in(keys[9], 71), 0)
    return {"displacement": displacement, "velocity": velocity, "shear": shear, "normals": normals, "gap_zero": gap_zero, "mortar": mortar, "owner": owner, "blocks": blocks, "live_rows": live_rows}


DAMPING = 0.9
TIME_STEP = 0.1
PENALTY = 10.0
LAME_RATIO = 2.0


def corner_sets(layer):
    return (layer[:, :, :-1, :-1], layer[:, :, 1:, :-1], layer[:, :, :-1, 1:], layer[:, :, 1:, 1:])


def element_forces(extended, shear, valid):
    lower = corner_sets(extended[:, :-1])
    upper = corner_sets(extended[:, 1:])
    grad_depth = 0.25 * (upper[0] + upper[1] + upper[2] + upper[3] - lower[0] - lower[1] - lower[2] - lower[3])
    grad_rows = 0.25 * (lower[1] + lower[3] + upper[1] + upper[3] - lower[0] - lower[2] - upper[0] - upper[2])
    grad_cols = 0.25 * (lower[2] + lower[3] + upper[2] + upper[3] - lower[0] - lower[1] - upper[0] - upper[1])
    grads = (grad_depth, grad_rows, grad_cols)
    deform = [[grads[col_d][row_c] + (1.0 if row_c == col_d else 0.0) for col_d in range(3)] for row_c in range(3)]
    cofactor = [[deform[(row_c + 1) % 3][(col_d + 1) % 3] * deform[(row_c + 2) % 3][(col_d + 2) % 3]
                 - deform[(row_c + 1) % 3][(col_d + 2) % 3] * deform[(row_c + 2) % 3][(col_d + 1) % 3]
                 for col_d in range(3)] for row_c in range(3)]
    jacobian = deform[0][0] * cofactor[0][0] + deform[0][1] * cofactor[0][1] + deform[0][2] * cofactor[0][2]
    modulus = shear * valid
    scaling = LAME_RATIO * modulus * (jacobian - 1.0) - modulus
    quarters = [jnp.stack([0.25 * (modulus * deform[row_c][col_d] + scaling * cofactor[row_c][col_d]) for row_c in range(3)], 0)
                for col_d in range(3)]
    total = jnp.zeros(extended.shape, jnp.float32)
    for off_depth in (0, 1):
        for off_rows in (0, 1):
            for off_cols in (0, 1):
                term = -((2 * off_depth - 1) * quarters[0] + (2 * off_rows - 1) * quarters[1] + (2 * off_cols - 1) * quarters[2])
                total = total + jnp.pad(term, ((0, 0), (off_depth, 1 - off_depth), (off_rows, 1 - off_rows), (off_cols, 1 - off_cols)))
    return total


def penalty(slave, master, facing, opening, coupling, live):
    projected = jnp.einsum("rij,crj->cri", coupling, master, precision=lax.Precision.HIGHEST)
    gap = opening + jnp.sum(facing * (slave - projected), axis=0)
    pressure = PENALTY * jnp.maximum(-gap, 0.0) * live[:, None]
    slave_force = pressure * facing
    reaction = -jnp.einsum("rij,cri->crj", coupling, slave_force, precision=lax.Precision.HIGHEST)
    return slave_force, reaction


def reference(displacement, velocity, shear, normals, gap_zero, mortar, owner, blocks, live_rows):
    index_rows = jnp.arange(ROWS)
    index_cols = jnp.arange(COLS)
    valid = ((index_rows < ROWS - 1)[:, None]
             & ((index_cols < COLS - 1) & (index_cols != COLS // 2 + BLOCK // 2 - 1))[None, :]).astype(jnp.float32)
    master_rows = (index_rows // ROWS_DEV * ROWS_DEV)[:, None] + blocks
    local_rows = index_rows % ROWS_DEV
    live = (local_rows[:, None] < jnp.repeat(live_rows, ROWS_DEV, axis=0)).astype(jnp.float32).reshape(ROWS * N_GY)
    coupling = mortar.astype(jnp.float32).reshape(ROWS * N_GY, BLOCK, BLOCK)
    facing = normals.reshape(3, ROWS * N_GY, BLOCK)
    opening = gap_zero.reshape(ROWS * N_GY, BLOCK)
    for iteration in range(STEPS):
        extended = jnp.pad(displacement, ((0, 0), (0, 0), (0, 1), (0, 1)))
        forces = element_forces(extended, shear, valid)[:, :, :ROWS, :COLS]
        surface = displacement[:, 0].reshape(3, ROWS, N_GY, BLOCK)
        masters = surface[:, master_rows, owner, :]
        slave_force, reaction = penalty(surface.reshape(3, ROWS * N_GY, BLOCK), masters.reshape(3, ROWS * N_GY, BLOCK),
                                        facing, opening, coupling, live)
        returned = jnp.zeros((3, ROWS, N_GY, BLOCK), jnp.float32).at[:, master_rows, owner, :].add(
            reaction.reshape(3, ROWS, N_GY, BLOCK))
        contact = (slave_force + returned.reshape(3, ROWS * N_GY, BLOCK)).reshape(3, ROWS, COLS)
        velocity = DAMPING * velocity + TIME_STEP * forces.at[:, 0].add(contact)
        displacement = displacement + TIME_STEP * velocity
    return displacement, velocity
```

```python
import functools

import jax
import jax.numpy as jnp
from jax import lax
from jax.experimental import pallas as pl
from jax.experimental.pallas import tpu as pltpu
from jax.sharding import PartitionSpec as P

STEPS = 2
DAMPING = 0.9
TIME_STEP = 0.1
PENALTY = 10.0
CHUNK = 16
DEAD = 4096
MESH = pl.DeviceIdType.MESH
F32 = jnp.float32
BF16 = jnp.bfloat16


def kernel(count_gx, count_gy, u_in, v_in, shear_in, normals_in, gap_in, mortar_in, index_in, u_out, v_out,
           ubuf, vbuf, mbuf, nbuf, gapbuf, mort, ibuf,
           f1buf, wbuf, c1buf, c2buf,
           row_send, row_recv, col_send, col_recv,
           rim_row_send, rim_row_recv, rim_col_send, rim_col_recv, rim_diag_recv,
           near, split, onehot, onehot_t, gathered, projected, forces_lhs, reacted, returned, relay_recv, combined,
           opp_recv, cross_recv, slave,
           load_sem, out_sem, send_sem, recv_sem):
    depth, rows, cols = u_in.shape[1:]
    me_x = lax.axis_index("gx")
    me_y = lax.axis_index("gy")
    half = count_gy // 2
    parity = lax.rem(me_y, 2)
    up_x = lax.rem(me_x + count_gx - 1, count_gx)
    down_x = lax.rem(me_x + 1, count_gx)
    up_y = lax.rem(me_y + count_gy - 1, count_gy)
    down_y = lax.rem(me_y + 1, count_gy)
    opposite = lax.rem(me_y + half, count_gy)
    cross = lax.rem(me_y + half - 1 + 2 * parity, count_gy)
    partner = me_y + 1 - 2 * parity

    loads = [
        pltpu.make_async_copy(u_in, ubuf.at[:, 0:depth, 0:rows, :], load_sem.at[0]),
        pltpu.make_async_copy(shear_in, mbuf.at[0:depth - 1], load_sem.at[1]),
        pltpu.make_async_copy(index_in, ibuf, load_sem.at[2]),
        pltpu.make_async_copy(v_in, vbuf, load_sem.at[3]),
        pltpu.make_async_copy(normals_in, nbuf, load_sem.at[4]),
        pltpu.make_async_copy(gap_in, gapbuf, load_sem.at[5]),
        pltpu.make_async_copy(mortar_in, mort, load_sem.at[6]),
    ]
    for load in loads:
        load.start()

    barrier = pltpu.get_barrier_semaphore()
    greeted = [(up_x, me_y), (down_x, me_y), (me_x, up_y), (me_x, down_y), (up_x, up_y), (down_x, down_y),
               (me_x, opposite), (me_x, cross)]
    for device in greeted:
        pl.semaphore_signal(barrier, inc=1, device_id=device, device_id_type=MESH)

    lane = lax.broadcasted_iota(jnp.int32, (CHUNK, cols), 1)
    first_lane = lane == 0
    last_lane = lane == cols - 1
    lane_full = lax.broadcasted_iota(jnp.int32, (rows, cols), 1)

    def send(step, slot, source, target, device):
        copy = pltpu.make_async_remote_copy(
            src_ref=source, dst_ref=target, send_sem=send_sem.at[step, slot], recv_sem=recv_sem.at[step, slot],
            device_id=device, device_id_type=MESH)
        copy.start()
        return copy

    def surface_sends(step, source):
        return (send(step, 0, source, near.at[step, 0], (me_x, opposite)),
                send(step, 1, source, near.at[step, 2], (me_x, cross)))

    for c in range(3):
        ubuf[c, depth] = jnp.zeros((rows + 8, cols), F32)
    c1buf[rows:rows + 8] = jnp.zeros((8, cols), F32)
    c2buf[0:8] = jnp.zeros((8, cols), F32)
    c2buf[rows + 8:rows + 16] = jnp.zeros((8, cols), F32)
    mbuf[depth - 1] = jnp.zeros((rows, cols), F32)
    col_send[rows:rows + 8] = jnp.zeros((8, cols), F32)

    pl.semaphore_wait(barrier, 8)
    pending = []
    first_surface = surface_sends(0, u_in.at[:, 0])

    def halo_sends(step):
        packed = jnp.zeros((rows, cols), F32)
        for c in range(3):
            for k in range(depth):
                idx = c * depth + k
                row_send[step, idx:idx + 1] = ubuf[c, k, 0:1]
                value = ubuf[c, k, 0:rows]
                moved = value if idx == 0 else pltpu.roll(value, idx, 1)
                packed = jnp.where(lane_full == idx, moved, packed)
        col_send[step * (rows + 8):step * (rows + 8) + rows] = packed
        base = step * (rows + 8)
        return (send(step, 2, row_send.at[step], row_recv.at[step], (up_x, me_y)),
                send(step, 3, col_send.at[base:base + rows], col_recv.at[step, 0:rows], (me_x, up_y)),
                send(step, 4, col_send.at[base:base + 8], col_recv.at[step, rows:rows + 8], (up_x, up_y)))

    loads[0].wait()
    first_halo = halo_sends(0)
    loads[1].wait()
    row_at = lax.broadcasted_iota(jnp.int32, (rows, cols), 0) + me_x * rows
    col_at = lane_full + me_y * cols
    valid = ((row_at < count_gx * rows - 1) & (col_at < count_gy * cols - 1)
             & (col_at != count_gy * cols // 2 + cols // 2 - 1))
    for k in range(depth - 1):
        mbuf[k] = jnp.where(valid, mbuf[k] * (1.0 / 16.0), 0.0)
    loads[2].wait()

    wide = 8 * rows
    raw = ibuf[0:wide]
    place = jnp.where(raw >= 0, raw, raw + DEAD)
    which = lax.rem(lax.broadcasted_iota(jnp.int32, (wide, cols), 0), 8)
    target = jnp.where(which < 6, which * (3 * rows) + place, -1)
    lane_wide = lax.broadcasted_iota(jnp.int32, (wide, cols), 1)
    for j in range(6 * 3 * rows // cols):
        onehot[:, j * cols:(j + 1) * cols] = jnp.where(lane_wide + j * cols == target, 1.0, 0.0).astype(BF16)
    raw_t = ibuf[wide:wide + 8][0:1]
    place_t = jnp.where(raw_t >= 0, raw_t, raw_t + DEAD)
    onehot_t[...] = jnp.where(
        lax.broadcasted_iota(jnp.int32, (3 * rows, cols), 0) == place_t, 1.0, 0.0).astype(BF16)
    live = ibuf[pl.ds(0, rows, stride=8)] >= 0

    for step in range(STEPS):
        if step == 0:
            surface, halo = first_surface, first_halo
        for copy in halo:
            copy.wait()
        for c in range(3):
            for k in range(depth):
                ubuf[c, k, rows:rows + 1] = row_recv[step, c * depth + k:c * depth + k + 1]

        def chunk_body(chunk, carry):
            r0 = pl.multiple_of(chunk * CHUNK, CHUNK)
            here = pl.ds(r0, CHUNK)
            below = pl.ds(r0 + 1, CHUNK)
            edge = col_recv[step, here]
            edge_below = col_recv[step, below]
            edge_sum = edge + edge_below
            edge_diff = edge_below - edge

            def shifted(value, side, idx):
                return jnp.where(last_lane, pltpu.roll(side, (cols - 1 - idx) % cols, 1), pltpu.roll(value, cols - 1, 1))

            def layer(k):
                out = []
                for c in range(3):
                    own = ubuf[c, k, here]
                    under = ubuf[c, k, below]
                    total = own + under
                    diff = under - own
                    idx = min(c * depth + k, 3 * depth - 1)
                    total_next = shifted(total, edge_sum, idx)
                    diff_next = shifted(diff, edge_diff, idx)
                    out.append((total + total_next, diff + diff_next, total_next - total))
                return out

            previous = layer(0)
            held = None
            pack1 = jnp.zeros((CHUNK, cols), F32)
            pack2 = jnp.zeros((CHUNK, cols), F32)
            for k in range(depth):
                if k < depth - 1:
                    current = layer(k + 1)
                    deform = [[current[c][0] - previous[c][0], previous[c][1] + current[c][1],
                               previous[c][2] + current[c][2]] for c in range(3)]
                    for c in range(3):
                        deform[c][c] = deform[c][c] + 4.0
                    previous = current
                    cofactor = [[deform[(c + 1) % 3][(d + 1) % 3] * deform[(c + 2) % 3][(d + 2) % 3]
                                 - deform[(c + 1) % 3][(d + 2) % 3] * deform[(c + 2) % 3][(d + 1) % 3]
                                 for d in range(3)] for c in range(3)]
                    jacobian = (deform[0][0] * cofactor[0][0] + deform[0][1] * cofactor[0][1]
                                + deform[0][2] * cofactor[0][2])
                    modulus = mbuf[k, here]
                    weight = modulus * (jacobian * (1.0 / 128.0) - 0.75)
                    quarter = [[modulus * deform[c][d] + weight * cofactor[c][d] for d in range(3)] for c in range(3)]
                for c in range(3):
                    if k == 0:
                        a, b, e = quarter[c]
                    elif k < depth - 1:
                        a = quarter[c][0] - held[c][0]
                        b = quarter[c][1] + held[c][1]
                        e = quarter[c][2] + held[c][2]
                    else:
                        a, b, e = -held[c][0], held[c][1], held[c][2]
                    plus = a + e
                    minus = a - e
                    z1 = minus + b
                    z2 = minus - b
                    idx = c * depth + k
                    f1buf[c, k, here] = (plus + b) + jnp.where(first_lane, 0.0, pltpu.roll(z1, 1, 1))
                    wbuf[c, k, pl.ds(r0 + 8, CHUNK)] = (plus - b) + jnp.where(first_lane, 0.0, pltpu.roll(z2, 1, 1))
                    pack1 = jnp.where(lane == idx, pltpu.roll(z1, idx + 1, 1), pack1)
                    pack2 = jnp.where(lane == idx, pltpu.roll(z2, idx + 1, 1), pack2)
                held = quarter
            c1buf[here] = pack1
            c2buf[pl.ds(r0 + 8, CHUNK)] = pack2
            return carry

        lax.fori_loop(0, rows // CHUNK, chunk_body, 0)
        for c in range(3):
            for k in range(depth):
                idx = c * depth + k
                rim_row_send[step, idx:idx + 1] = wbuf[c, k, rows + 7:rows + 8]
        rim_col_send[step] = c1buf[0:rows + 8] + c2buf[7:rows + 15]
        rims = (send(step, 5, rim_row_send.at[step], rim_row_recv.at[step], (down_x, me_y)),
                send(step, 6, rim_col_send.at[step, 0:rows], rim_col_recv.at[step], (me_x, down_y)),
                send(step, 7, rim_col_send.at[step, rows:rows + 8], rim_diag_recv.at[step], (down_x, down_y)))

        surface[0].wait()
        relay = send(step, 8, near.at[step, 0], near.at[step, 1], (me_x, partner))

        def split_slot(slot):
            for c in range(3):
                value = near[step, slot, c]
                high = value.astype(BF16)
                low = (value - high.astype(F32)).astype(BF16)
                split[c * 3 * rows + slot * rows:c * 3 * rows + (slot + 1) * rows] = high
                split[(c + 3) * 3 * rows + slot * rows:(c + 3) * 3 * rows + (slot + 1) * rows] = low

        split_slot(0)
        surface[1].wait()
        split_slot(2)
        relay.wait()
        split_slot(1)
        gathered[...] = jnp.dot(onehot[...], split[...], preferred_element_type=F32).astype(BF16)
        if step == 0:
            for load in loads[4:7]:
                load.wait()

        group = 8

        def project(i, carry):
            for g in range(group):
                pair = i * group + g
                at16 = pl.multiple_of(pair * 16, 16)
                couple = mort[pl.ds(pl.multiple_of(pair * 2 * cols, 2 * cols), 2 * cols)]
                result = lax.dot_general(gathered[pl.ds(at16, 16)], couple, (((1,), (1,)), ((), ())),
                                         preferred_element_type=F32)
                projected[pl.ds(at16, 8)] = result[0:8, 0:cols]
                projected[pl.ds(at16 + 8, 8)] = result[8:16, cols:2 * cols]
            return carry

        lax.fori_loop(0, rows // 2 // group, project, 0)
        gap = gapbuf[...]
        for c in range(3):
            shadow = projected[pl.ds(c, rows, stride=8)] + projected[pl.ds(c + 3, rows, stride=8)]
            gap = gap + nbuf[c] * (ubuf[c, 0, 0:rows] - shadow)
        pressure = jnp.where(live, PENALTY * jnp.maximum(-gap, 0.0), 0.0)
        for c in range(3):
            force = pressure * nbuf[c]
            slave[c] = force
            high = force.astype(BF16).astype(F32)
            forces_lhs[pl.ds(c, rows, stride=8)] = high
            forces_lhs[pl.ds(c + 3, rows, stride=8)] = force - high
            if c < 2:
                forces_lhs[pl.ds(c + 6, rows, stride=8)] = jnp.zeros((rows, cols), F32)

        upper = lax.broadcasted_iota(jnp.int32, (16, cols), 0) < 8

        def react(i, carry):
            for g in range(group):
                pair = i * group + g
                at16 = pl.multiple_of(pair * 16, 16)
                couple = mort[pl.ds(pl.multiple_of(pair * 2 * cols, 2 * cols), 2 * cols)]
                both = forces_lhs[pl.ds(at16, 16)]
                left = jnp.concatenate([jnp.where(upper, both, 0.0), jnp.where(upper, 0.0, both)], 1).astype(BF16)
                reacted[pl.ds(at16, 16)] = jnp.dot(left, couple, preferred_element_type=F32)
            return carry

        lax.fori_loop(0, rows // 2 // group, react, 0)
        highs, lows = [], []
        for c in range(3):
            value = -(reacted[pl.ds(c, rows, stride=8)] + reacted[pl.ds(c + 3, rows, stride=8)])
            high = value.astype(BF16)
            highs.append(high)
            lows.append((value - high.astype(F32)).astype(BF16))
        stack = jnp.concatenate([jnp.concatenate(highs, 1), jnp.concatenate(lows, 1)], 0)
        scattered = jnp.dot(onehot_t[...], stack, preferred_element_type=F32)
        for slot in (1, 2, 0):
            for c in range(3):
                returned[step, slot, c] = scattered[slot * rows:(slot + 1) * rows, c * cols:(c + 1) * cols]
        back_relay = send(step, 9, returned.at[step, 1], relay_recv.at[step], (me_x, partner))
        back_cross = send(step, 10, returned.at[step, 2], cross_recv.at[step], (me_x, cross))
        back_relay.wait()
        for c in range(3):
            combined[step, c] = returned[step, 0, c] + relay_recv[step, c]
        back_opp = send(step, 11, combined.at[step], opp_recv.at[step], (me_x, opposite))

        for copy in rims:
            copy.wait()
        if step == 0:
            loads[3].wait()
        corner = jnp.where(lax.broadcasted_iota(jnp.int32, (8, cols), 0) == 0, rim_diag_recv[step], 0.0)
        rim_col_recv[step, 0:8] = rim_col_recv[step, 0:8] + corner

        def update(k, extra):
            for c in range(3):
                idx = c * depth + k
                wbuf[c, k, 7:8] = rim_row_recv[step, idx:idx + 1]
                force = f1buf[c, k] + wbuf[c, k, 7:rows + 7]
                side = rim_col_recv[step]
                side = side if idx == 0 else pltpu.roll(side, cols - idx, 1)
                force = force + jnp.where(lane_full == 0, side, 0.0)
                if extra is not None:
                    force = force + extra[c]
                speed = DAMPING * vbuf[c, k] + TIME_STEP * force
                vbuf[c, k] = speed
                ubuf[c, k, 0:rows] = ubuf[c, k, 0:rows] + TIME_STEP * speed

        for k in range(1, depth):
            update(k, None)
        outs = []
        if step == STEPS - 1:
            outs = [pltpu.make_async_copy(vbuf.at[:, 1:depth], v_out.at[:, 1:depth], out_sem.at[0]),
                    pltpu.make_async_copy(ubuf.at[:, 1:depth, 0:rows], u_out.at[:, 1:depth], out_sem.at[1])]
            for copy in outs:
                copy.start()
        back_cross.wait()
        back_opp.wait()
        update(0, [slave[c] + opp_recv[step, c] + cross_recv[step, c] for c in range(3)])
        if step == STEPS - 1:
            last = [pltpu.make_async_copy(vbuf.at[:, 0], v_out.at[:, 0], out_sem.at[2]),
                    pltpu.make_async_copy(ubuf.at[:, 0, 0:rows], u_out.at[:, 0], out_sem.at[3])]
            for copy in last:
                copy.start()
            for copy in outs + last:
                copy.wait()
        else:
            surface = surface_sends(step + 1, ubuf.at[:, 0, 0:rows])
            halo = halo_sends(step + 1)


def local(count_gx, count_gy, displacement, velocity, shear, normals, gap_zero, mortar, owner, blocks, live_rows):
    _, depth, rows, cols = displacement.shape
    column = lax.axis_index("gy")
    parity = lax.rem(column, 2)
    ahead = owner[:, 0] - lax.rem(column + count_gy // 2, count_gy) + 1
    ahead = jnp.where(ahead < 0, ahead + count_gy, jnp.where(ahead >= count_gy, ahead - count_gy, ahead))
    side = (ahead - 1) * (1 - 2 * parity)
    place = jnp.where(side < 0, 2, side) * rows + blocks[:, 0]
    place = jnp.where(jnp.arange(rows, dtype=jnp.int32) < live_rows[0, 0], place, place - DEAD)
    index = jnp.concatenate([jnp.broadcast_to(jnp.repeat(place, 8)[:, None], (8 * rows, cols)),
                             jnp.broadcast_to(jnp.tile(place, cols // rows)[None], (8, cols))], 0)
    any_space = pl.BlockSpec(memory_space=pl.ANY)
    vmem = pltpu.VMEM
    two = STEPS
    lines = 3 * depth
    scratch = [
        vmem((3, depth + 1, rows + 8, cols), F32), vmem((3, depth, rows, cols), F32), vmem((depth, rows, cols), F32),
        vmem((3, rows, cols), F32), vmem((rows, cols), F32), vmem((rows * cols, cols), BF16),
        vmem((8 * rows + 8, cols), jnp.int32),
        vmem((3, depth, rows, cols), F32), vmem((3, depth, rows + 8, cols), F32), vmem((rows + 8, cols), F32),
        vmem((rows + 16, cols), F32),
        vmem((two, lines, cols), F32), vmem((two, lines, cols), F32), vmem((two * (rows + 8), cols), F32),
        vmem((two, rows + 8, cols), F32),
        vmem((two, lines, cols), F32), vmem((two, lines, cols), F32), vmem((two, rows + 8, cols), F32),
        vmem((two, rows, cols), F32), vmem((two, 8, cols), F32),
        vmem((two, 3, 3, rows, cols), F32), vmem((18 * rows, cols), BF16), vmem((8 * rows, 18 * rows), BF16),
        vmem((3 * rows, cols), BF16), vmem((8 * rows, cols), BF16), vmem((8 * rows, cols), F32),
        vmem((8 * rows, cols), F32), vmem((8 * rows, cols), F32), vmem((two, 3, 3, rows, cols), F32),
        vmem((two, 3, rows, cols), F32), vmem((two, 3, rows, cols), F32),
        vmem((two, 3, rows, cols), F32), vmem((two, 3, rows, cols), F32), vmem((3, rows, cols), F32),
        pltpu.SemaphoreType.DMA((7,)), pltpu.SemaphoreType.DMA((4,)),
        pltpu.SemaphoreType.DMA((two, 12)), pltpu.SemaphoreType.DMA((two, 12)),
    ]
    return pl.pallas_call(
        functools.partial(kernel, count_gx, count_gy),
        out_shape=(jax.ShapeDtypeStruct(displacement.shape, F32), jax.ShapeDtypeStruct(velocity.shape, F32)),
        in_specs=[any_space] * 7,
        out_specs=(any_space, any_space),
        scratch_shapes=scratch,
        compiler_params=pltpu.CompilerParams(collective_id=0, has_side_effects=True, vmem_limit_bytes=48 << 20),
    )(displacement, velocity, shear, normals, gap_zero, mortar.reshape(rows * cols, cols), index)


def solution(mesh):
    in_specs = (
        P(None, None, "gx", "gy"),
        P(None, None, "gx", "gy"),
        P(None, "gx", "gy"),
        P(None, "gx", "gy"),
        P("gx", "gy"),
        P("gx", "gy", None, None),
        P("gx", "gy"),
        P("gx", "gy"),
        P("gx", "gy"),
    )
    out_specs = (P(None, None, "gx", "gy"), P(None, None, "gx", "gy"))
    step = functools.partial(local, mesh.shape["gx"], mesh.shape["gy"])
    return jax.shard_map(step, mesh=mesh, in_specs=in_specs, out_specs=out_specs, check_vma=False)
```

```python
import functools

import jax
import jax.numpy as jnp
from jax import lax
from jax.experimental import pallas as pl
from jax.experimental.pallas import tpu as pltpu
from jax.sharding import PartitionSpec as P

STEPS = 2
DAMPING = 0.9
TIME_STEP = 0.1
PENALTY = 10.0
CHUNK = 16
DEAD = 4096
MESH = pl.DeviceIdType.MESH
F32 = jnp.float32
BF16 = jnp.bfloat16


def kernel(count_gx, count_gy, u_in, v_in, shear_in, normals_in, gap_in, mortar_in, index_in, u_out, v_out,
           ubuf, vbuf, mbuf, nbuf, gapbuf, mort, ibuf,
           f1buf, wbuf, c1buf, c2buf,
           row_send, row_recv, col_send, col_recv,
           rim_row_send, rim_row_recv, rim_col_send, rim_col_recv, rim_diag_recv,
           near, split, onehot, onehot_t, gathered, projected, forces_lhs, reacted, returned, relay_recv, combined,
           opp_recv, cross_recv, slave,
           load_sem, out_sem, send_sem, recv_sem):
    depth, rows, cols = u_in.shape[1:]
    me_x = lax.axis_index("gx")
    me_y = lax.axis_index("gy")
    half = count_gy // 2
    parity = lax.rem(me_y, 2)
    up_x = lax.rem(me_x + count_gx - 1, count_gx)
    down_x = lax.rem(me_x + 1, count_gx)
    up_y = lax.rem(me_y + count_gy - 1, count_gy)
    down_y = lax.rem(me_y + 1, count_gy)
    opposite = lax.rem(me_y + half, count_gy)
    cross = lax.rem(me_y + half - 1 + 2 * parity, count_gy)
    partner = me_y + 1 - 2 * parity
    beside = lax.rem(me_y + count_gy - 1 + 2 * parity, count_gy)
    spot = lax.rem(me_y, half)
    direct = (spot == 0) | (spot == half - 1)
    relayed = jnp.logical_not(direct)
    cross_way = jnp.where(direct, cross, beside)

    loads = [
        pltpu.make_async_copy(u_in, ubuf.at[:, 0:depth, 0:rows, :], load_sem.at[0]),
        pltpu.make_async_copy(shear_in, mbuf.at[0:depth - 1], load_sem.at[1]),
        pltpu.make_async_copy(index_in, ibuf, load_sem.at[2]),
        pltpu.make_async_copy(v_in, vbuf, load_sem.at[3]),
        pltpu.make_async_copy(normals_in, nbuf, load_sem.at[4]),
        pltpu.make_async_copy(gap_in, gapbuf, load_sem.at[5]),
        pltpu.make_async_copy(mortar_in, mort, load_sem.at[6]),
    ]
    for load in loads:
        load.start()

    barrier = pltpu.get_barrier_semaphore()
    greeted = [(up_x, me_y), (down_x, me_y), (me_x, up_y), (me_x, down_y), (up_x, up_y), (down_x, down_y),
               (me_x, opposite), (me_x, cross)]
    for device in greeted:
        pl.semaphore_signal(barrier, inc=1, device_id=device, device_id_type=MESH)

    lane = lax.broadcasted_iota(jnp.int32, (CHUNK, cols), 1)
    first_lane = lane == 0
    last_lane = lane == cols - 1
    lane_full = lax.broadcasted_iota(jnp.int32, (rows, cols), 1)

    def describe(step, slot, source, target, device):
        return pltpu.make_async_remote_copy(
            src_ref=source, dst_ref=target, send_sem=send_sem.at[step, slot], recv_sem=recv_sem.at[step, slot],
            device_id=device, device_id_type=MESH)

    def send(step, slot, source, target, device):
        copy = describe(step, slot, source, target, device)
        copy.start()
        return copy

    def cross_send(step, c, source, device):
        return describe(step, 9 + c, source, near.at[step, 2, c], (me_x, device))

    def surface_sends(step, source):
        out = []
        for c in range(3):
            out.append(send(step, 6 + c, source.at[c], near.at[step, 0, c], (me_x, opposite)))

        @pl.when(direct)
        def _():
            for c in range(3):
                cross_send(step, c, source.at[c], cross).start()
        return out

    for c in range(3):
        ubuf[c, depth] = jnp.zeros((rows + 8, cols), F32)
    c1buf[rows:rows + 8] = jnp.zeros((8, cols), F32)
    c2buf[0:8] = jnp.zeros((8, cols), F32)
    c2buf[rows + 8:rows + 16] = jnp.zeros((8, cols), F32)
    mbuf[depth - 1] = jnp.zeros((rows, cols), F32)

    def halo_pack(step, layers, fresh):
        base = step * (rows + 8)
        packed = jnp.zeros((rows, cols), F32) if fresh else col_send[base:base + rows]
        for c in range(3):
            for k in layers:
                idx = c * depth + k
                row_send[step, idx:idx + 1] = ubuf[c, k, 0:1]
                value = ubuf[c, k, 0:rows]
                moved = value if idx == 0 else pltpu.roll(value, idx, 1)
                packed = jnp.where(lane_full == idx, moved, packed)
        col_send[base:base + rows] = packed

    def halo_sends(step):
        base = step * (rows + 8)
        return (send(step, 0, row_send.at[step], row_recv.at[step], (up_x, me_y)),
                send(step, 1, col_send.at[base:base + rows], col_recv.at[step, 0:rows], (me_x, up_y)),
                send(step, 2, col_send.at[base:base + 8], col_recv.at[step, rows:rows + 8], (up_x, up_y)))

    loads[0].wait()
    halo_pack(0, range(depth), True)
    pl.semaphore_wait(barrier, 8)
    halo = halo_sends(0)
    surface = surface_sends(0, u_in.at[:, 0])
    loads[1].wait()
    row_at = lax.broadcasted_iota(jnp.int32, (rows, cols), 0) + me_x * rows
    col_at = lane_full + me_y * cols
    valid = ((row_at < count_gx * rows - 1) & (col_at < count_gy * cols - 1)
             & (col_at != count_gy * cols // 2 + cols // 2 - 1))
    for k in range(depth - 1):
        mbuf[k] = jnp.where(valid, mbuf[k] * (1.0 / 16.0), 0.0)
    loads[2].wait()

    wide = 8 * rows
    raw = ibuf[0:wide]
    place = jnp.where(raw >= 0, raw, raw + DEAD)
    which = lax.rem(lax.broadcasted_iota(jnp.int32, (wide, cols), 0), 8)
    target = jnp.where(which < 6, which * (3 * rows) + place, -1)
    lane_wide = lax.broadcasted_iota(jnp.int32, (wide, cols), 1)
    for j in range(6 * 3 * rows // cols):
        onehot[:, j * cols:(j + 1) * cols] = jnp.where(lane_wide + j * cols == target, 1.0, 0.0).astype(BF16)
    raw_t = ibuf[wide:wide + 8][0:1]
    place_t = jnp.where(raw_t >= 0, raw_t, raw_t + DEAD)
    onehot_t[...] = jnp.where(
        lax.broadcasted_iota(jnp.int32, (3 * rows, cols), 0) == place_t, 1.0, 0.0).astype(BF16)
    live = ibuf[pl.ds(0, rows, stride=8)] >= 0

    for step in range(STEPS):
        for copy in halo:
            copy.wait()
        for c in range(3):
            for k in range(depth):
                ubuf[c, k, rows:rows + 1] = row_recv[step, c * depth + k:c * depth + k + 1]

        def chunk_body(chunk):
            r0 = chunk * CHUNK
            here = pl.ds(r0, CHUNK)
            below = pl.ds(r0 + 1, CHUNK)
            edge = col_recv[step, here]
            edge_below = col_recv[step, below]
            edge_sum = edge + edge_below
            edge_diff = edge_below - edge

            def shifted(value, side, idx):
                return jnp.where(last_lane, pltpu.roll(side, (cols - 1 - idx) % cols, 1), pltpu.roll(value, cols - 1, 1))

            def layer(k):
                out = []
                for c in range(3):
                    own = ubuf[c, k, here]
                    under = ubuf[c, k, below]
                    total = own + under
                    diff = under - own
                    idx = min(c * depth + k, 3 * depth - 1)
                    total_next = shifted(total, edge_sum, idx)
                    diff_next = shifted(diff, edge_diff, idx)
                    out.append((total + total_next, diff + diff_next, total_next - total))
                return out

            previous = layer(0)
            held = None
            pack1 = jnp.zeros((CHUNK, cols), F32)
            pack2 = jnp.zeros((CHUNK, cols), F32)
            for k in range(depth):
                if k < depth - 1:
                    current = layer(k + 1)
                    deform = [[current[c][0] - previous[c][0], previous[c][1] + current[c][1],
                               previous[c][2] + current[c][2]] for c in range(3)]
                    for c in range(3):
                        deform[c][c] = deform[c][c] + 4.0
                    previous = current
                    cofactor = [[deform[(c + 1) % 3][(d + 1) % 3] * deform[(c + 2) % 3][(d + 2) % 3]
                                 - deform[(c + 1) % 3][(d + 2) % 3] * deform[(c + 2) % 3][(d + 1) % 3]
                                 for d in range(3)] for c in range(3)]
                    jacobian = (deform[0][0] * cofactor[0][0] + deform[0][1] * cofactor[0][1]
                                + deform[0][2] * cofactor[0][2])
                    modulus = mbuf[k, here]
                    weight = modulus * (jacobian * (1.0 / 128.0) - 0.75)
                    quarter = [[modulus * deform[c][d] + weight * cofactor[c][d] for d in range(3)] for c in range(3)]
                for c in range(3):
                    if k == 0:
                        a, b, e = quarter[c]
                    elif k < depth - 1:
                        a = quarter[c][0] - held[c][0]
                        b = quarter[c][1] + held[c][1]
                        e = quarter[c][2] + held[c][2]
                    else:
                        a, b, e = -held[c][0], held[c][1], held[c][2]
                    plus = a + e
                    minus = a - e
                    z1 = minus + b
                    z2 = minus - b
                    idx = c * depth + k
                    f1buf[c, k, here] = (plus + b) + jnp.where(first_lane, 0.0, pltpu.roll(z1, 1, 1))
                    wbuf[c, k, pl.ds(r0 + 8, CHUNK)] = (plus - b) + jnp.where(first_lane, 0.0, pltpu.roll(z2, 1, 1))
                    pack1 = jnp.where(lane == idx, pltpu.roll(z1, idx + 1, 1), pack1)
                    pack2 = jnp.where(lane == idx, pltpu.roll(z2, idx + 1, 1), pack2)
                held = quarter
            c1buf[here] = pack1
            c2buf[pl.ds(r0 + 8, CHUNK)] = pack2

        relay = []

        def forward(c):
            surface[c].wait()
            relay.append(send(step, 12 + c, near.at[step, 0, c], near.at[step, 1, c], (me_x, partner)))

            @pl.when(relayed)
            def _():
                cross_send(step, c, near.at[step, 0, c], beside).start()

        chunks = rows // CHUNK
        for chunk in range(chunks):
            chunk_body(chunk)
            if chunk >= chunks - 3:
                forward(chunk - (chunks - 3))
        for c in range(3):
            for k in range(depth):
                idx = c * depth + k
                rim_row_send[step, idx:idx + 1] = wbuf[c, k, rows + 7:rows + 8]
        rim_col_send[step] = c1buf[0:rows + 8] + c2buf[7:rows + 15]
        rims = (send(step, 3, rim_row_send.at[step], rim_row_recv.at[step], (down_x, me_y)),
                send(step, 4, rim_col_send.at[step, 0:rows], rim_col_recv.at[step], (me_x, down_y)),
                send(step, 5, rim_col_send.at[step, rows:rows + 8], rim_diag_recv.at[step], (down_x, down_y)))

        def split_slot(slot):
            for c in range(3):
                value = near[step, slot, c]
                high = value.astype(BF16)
                low = (value - high.astype(F32)).astype(BF16)
                split[c * 3 * rows + slot * rows:c * 3 * rows + (slot + 1) * rows] = high
                split[(c + 3) * 3 * rows + slot * rows:(c + 3) * 3 * rows + (slot + 1) * rows] = low

        split_slot(0)
        for copy in relay:
            copy.wait()
        split_slot(1)
        for c in range(3):
            cross_send(step, c, near.at[step, 0, c], cross_way).wait()
        split_slot(2)
        gathered[...] = jnp.dot(onehot[...], split[...], preferred_element_type=F32).astype(BF16)
        if step == 0:
            for load in loads[4:7]:
                load.wait()

        group = 8

        def project(i, carry):
            for g in range(group):
                pair = i * group + g
                at16 = pl.multiple_of(pair * 16, 16)
                couple = mort[pl.ds(pl.multiple_of(pair * 2 * cols, 2 * cols), 2 * cols)]
                result = lax.dot_general(gathered[pl.ds(at16, 16)], couple, (((1,), (1,)), ((), ())),
                                         preferred_element_type=F32)
                projected[pl.ds(at16, 8)] = result[0:8, 0:cols]
                projected[pl.ds(at16 + 8, 8)] = result[8:16, cols:2 * cols]
            return carry

        lax.fori_loop(0, rows // 2 // group, project, 0)
        gap = gapbuf[...]
        for c in range(3):
            shadow = projected[pl.ds(c, rows, stride=8)] + projected[pl.ds(c + 3, rows, stride=8)]
            gap = gap + nbuf[c] * (ubuf[c, 0, 0:rows] - shadow)
        pressure = jnp.where(live, PENALTY * jnp.maximum(-gap, 0.0), 0.0)
        for c in range(3):
            force = pressure * nbuf[c]
            slave[c] = force
            high = force.astype(BF16).astype(F32)
            forces_lhs[pl.ds(c, rows, stride=8)] = high
            forces_lhs[pl.ds(c + 3, rows, stride=8)] = force - high
            if c < 2:
                forces_lhs[pl.ds(c + 6, rows, stride=8)] = jnp.zeros((rows, cols), F32)

        upper = lax.broadcasted_iota(jnp.int32, (16, cols), 0) < 8

        def react(i, carry):
            for g in range(group):
                pair = i * group + g
                at16 = pl.multiple_of(pair * 16, 16)
                couple = mort[pl.ds(pl.multiple_of(pair * 2 * cols, 2 * cols), 2 * cols)]
                both = forces_lhs[pl.ds(at16, 16)]
                left = jnp.concatenate([jnp.where(upper, both, 0.0), jnp.where(upper, 0.0, both)], 1).astype(BF16)
                reacted[pl.ds(at16, 16)] = jnp.dot(left, couple, preferred_element_type=F32)
            return carry

        lax.fori_loop(0, rows // 2 // group, react, 0)
        highs, lows = [], []
        for c in range(3):
            value = -(reacted[pl.ds(c, rows, stride=8)] + reacted[pl.ds(c + 3, rows, stride=8)])
            high = value.astype(BF16)
            highs.append(high)
            lows.append((value - high.astype(F32)).astype(BF16))
        stack = jnp.concatenate([jnp.concatenate(highs, 1), jnp.concatenate(lows, 1)], 0)
        scattered = jnp.dot(onehot_t[...], stack, preferred_element_type=F32)
        for slot in (1, 2, 0):
            for c in range(3):
                returned[step, slot, c] = scattered[slot * rows:(slot + 1) * rows, c * cols:(c + 1) * cols]
        back_partner = [send(step, 15 + c, returned.at[step, 1, c], relay_recv.at[step, c], (me_x, partner))
                        for c in range(3)]
        back_cross = [send(step, 18 + c, returned.at[step, 2, c], cross_recv.at[step, c], (me_x, cross_way))
                      for c in range(3)]
        back_opp = []
        for c in range(3):
            back_partner[c].wait()
            combined[step, c] = returned[step, 0, c] + relay_recv[step, c]

            @pl.when(relayed)
            def _():
                back_cross[c].wait()
                combined[step, c] = combined[step, c] + cross_recv[step, c]
            back_opp.append(send(step, 21 + c, combined.at[step, c], opp_recv.at[step, c], (me_x, opposite)))

        for copy in rims:
            copy.wait()
        if step == 0:
            loads[3].wait()
        corner = jnp.where(lax.broadcasted_iota(jnp.int32, (8, cols), 0) == 0, rim_diag_recv[step], 0.0)
        rim_col_recv[step, 0:8] = rim_col_recv[step, 0:8] + corner

        def update(k, extra):
            for c in range(3):
                idx = c * depth + k
                wbuf[c, k, 7:8] = rim_row_recv[step, idx:idx + 1]
                force = f1buf[c, k] + wbuf[c, k, 7:rows + 7]
                side = rim_col_recv[step]
                side = side if idx == 0 else pltpu.roll(side, cols - idx, 1)
                force = force + jnp.where(lane_full == 0, side, 0.0)
                if extra is not None:
                    force = force + extra[c]
                speed = DAMPING * vbuf[c, k] + TIME_STEP * force
                vbuf[c, k] = speed
                ubuf[c, k, 0:rows] = ubuf[c, k, 0:rows] + TIME_STEP * speed

        for k in range(1, depth):
            update(k, None)
        outs = []
        if step == STEPS - 1:
            outs = [pltpu.make_async_copy(vbuf.at[:, 1:depth], v_out.at[:, 1:depth], out_sem.at[0]),
                    pltpu.make_async_copy(ubuf.at[:, 1:depth, 0:rows], u_out.at[:, 1:depth], out_sem.at[1])]
            for copy in outs:
                copy.start()
        else:
            halo_pack(step + 1, range(1, depth), True)

        @pl.when(direct)
        def _():
            for copy in back_cross:
                copy.wait()
        for copy in back_opp:
            copy.wait()
        update(0, [slave[c] + opp_recv[step, c] + jnp.where(direct, cross_recv[step, c], 0.0) for c in range(3)])
        if step == STEPS - 1:
            last = [pltpu.make_async_copy(vbuf.at[:, 0], v_out.at[:, 0], out_sem.at[2]),
                    pltpu.make_async_copy(ubuf.at[:, 0, 0:rows], u_out.at[:, 0], out_sem.at[3])]
            for copy in last:
                copy.start()
            for copy in outs + last:
                copy.wait()
        else:
            halo_pack(step + 1, range(1), False)
            halo = halo_sends(step + 1)
            surface = surface_sends(step + 1, ubuf.at[:, 0, 0:rows])


def local(count_gx, count_gy, displacement, velocity, shear, normals, gap_zero, mortar, owner, blocks, live_rows):
    _, depth, rows, cols = displacement.shape
    column = lax.axis_index("gy")
    parity = lax.rem(column, 2)
    ahead = owner[:, 0] - lax.rem(column + count_gy // 2, count_gy) + 1
    ahead = jnp.where(ahead < 0, ahead + count_gy, jnp.where(ahead >= count_gy, ahead - count_gy, ahead))
    side = (ahead - 1) * (1 - 2 * parity)
    place = jnp.where(side < 0, 2, side) * rows + blocks[:, 0]
    place = jnp.where(jnp.arange(rows, dtype=jnp.int32) < live_rows[0, 0], place, place - DEAD)
    index = jnp.concatenate([jnp.broadcast_to(jnp.repeat(place, 8)[:, None], (8 * rows, cols)),
                             jnp.broadcast_to(jnp.tile(place, cols // rows)[None], (8, cols))], 0)
    any_space = pl.BlockSpec(memory_space=pl.ANY)
    vmem = pltpu.VMEM
    two = STEPS
    lines = 3 * depth
    scratch = [
        vmem((3, depth + 1, rows + 8, cols), F32), vmem((3, depth, rows, cols), F32), vmem((depth, rows, cols), F32),
        vmem((3, rows, cols), F32), vmem((rows, cols), F32), vmem((rows * cols, cols), BF16),
        vmem((8 * rows + 8, cols), jnp.int32),
        vmem((3, depth, rows, cols), F32), vmem((3, depth, rows + 8, cols), F32), vmem((rows + 8, cols), F32),
        vmem((rows + 16, cols), F32),
        vmem((two, lines, cols), F32), vmem((two, lines, cols), F32), vmem((two * (rows + 8), cols), F32),
        vmem((two, rows + 8, cols), F32),
        vmem((two, lines, cols), F32), vmem((two, lines, cols), F32), vmem((two, rows + 8, cols), F32),
        vmem((two, rows, cols), F32), vmem((two, 8, cols), F32),
        vmem((two, 3, 3, rows, cols), F32), vmem((18 * rows, cols), BF16), vmem((8 * rows, 18 * rows), BF16),
        vmem((3 * rows, cols), BF16), vmem((8 * rows, cols), BF16), vmem((8 * rows, cols), F32),
        vmem((8 * rows, cols), F32), vmem((8 * rows, cols), F32), vmem((two, 3, 3, rows, cols), F32),
        vmem((two, 3, rows, cols), F32), vmem((two, 3, rows, cols), F32),
        vmem((two, 3, rows, cols), F32), vmem((two, 3, rows, cols), F32), vmem((3, rows, cols), F32),
        pltpu.SemaphoreType.DMA((7,)), pltpu.SemaphoreType.DMA((4,)),
        pltpu.SemaphoreType.DMA((two, 24)), pltpu.SemaphoreType.DMA((two, 24)),
    ]
    return pl.pallas_call(
        functools.partial(kernel, count_gx, count_gy),
        out_shape=(jax.ShapeDtypeStruct(displacement.shape, F32), jax.ShapeDtypeStruct(velocity.shape, F32)),
        in_specs=[pl.BlockSpec(memory_space=pltpu.HBM)] * 7,
        out_specs=(any_space, any_space),
        scratch_shapes=scratch,
        compiler_params=pltpu.CompilerParams(collective_id=0, has_side_effects=True, vmem_limit_bytes=48 << 20),
    )(*[pltpu.with_memory_space_constraint(x, pltpu.HBM) for x in (displacement, velocity, shear, normals, gap_zero, mortar.reshape(rows * cols, cols))], index)


def solution(mesh):
    in_specs = (
        P(None, None, "gx", "gy"),
        P(None, None, "gx", "gy"),
        P(None, "gx", "gy"),
        P(None, "gx", "gy"),
        P("gx", "gy"),
        P("gx", "gy", None, None),
        P("gx", "gy"),
        P("gx", "gy"),
        P("gx", "gy"),
    )
    out_specs = (P(None, None, "gx", "gy"), P(None, None, "gx", "gy"))
    step = functools.partial(local, mesh.shape["gx"], mesh.shape["gy"])
    return jax.shard_map(step, mesh=mesh, in_specs=in_specs, out_specs=out_specs, check_vma=False)
```

```python
import functools

import jax
import jax.numpy as jnp
from jax import lax
from jax.experimental import pallas as pl
from jax.experimental.pallas import tpu as pltpu
from jax.sharding import PartitionSpec as P

STEPS = 2
DAMPING = 0.9
TIME_STEP = 0.1
PENALTY = 10.0
CHUNK = 16
DEAD = 4096
MESH = pl.DeviceIdType.MESH
F32 = jnp.float32
BF16 = jnp.bfloat16


def kernel(count_gx, count_gy, u_in, v_in, shear_in, normals_in, gap_in, mortar_in, index_in, u_out, v_out,
           ubuf, vbuf, mbuf, nbuf, gapbuf, mort, ibuf,
           f1buf, wbuf, c1buf, c2buf,
           row_send, row_recv, col_send, col_recv,
           rim_row_send, rim_row_recv, rim_col_send, rim_col_recv, rim_diag_recv,
           near, split, onehot, onehot_t, gathered, projected, forces_lhs, reacted, returned, relay_recv, combined,
           opp_recv, cross_recv, slave,
           load_sem, out_sem, send_sem, recv_sem):
    depth, rows, cols = u_in.shape[1:]
    me_x = lax.axis_index("gx")
    me_y = lax.axis_index("gy")
    half = count_gy // 2
    parity = lax.rem(me_y, 2)
    up_x = lax.rem(me_x + count_gx - 1, count_gx)
    down_x = lax.rem(me_x + 1, count_gx)
    up_y = lax.rem(me_y + count_gy - 1, count_gy)
    down_y = lax.rem(me_y + 1, count_gy)
    opposite = lax.rem(me_y + half, count_gy)
    cross = lax.rem(me_y + half - 1 + 2 * parity, count_gy)
    partner = me_y + 1 - 2 * parity
    beside = lax.rem(me_y + count_gy - 1 + 2 * parity, count_gy)
    spot = lax.rem(me_y, half)
    direct = (spot == 0) | (spot == half - 1)
    relayed = jnp.logical_not(direct)
    cross_way = jnp.where(direct, cross, beside)

    loads = [
        pltpu.make_async_copy(u_in, ubuf.at[:, 0:depth, 0:rows, :], load_sem.at[0]),
        pltpu.make_async_copy(shear_in, mbuf.at[0:depth - 1], load_sem.at[1]),
        pltpu.make_async_copy(index_in, ibuf, load_sem.at[2]),
        pltpu.make_async_copy(v_in, vbuf, load_sem.at[3]),
        pltpu.make_async_copy(normals_in, nbuf, load_sem.at[4]),
        pltpu.make_async_copy(gap_in, gapbuf, load_sem.at[5]),
        pltpu.make_async_copy(mortar_in, mort, load_sem.at[6]),
    ]
    for load in loads:
        load.start()

    barrier = pltpu.get_barrier_semaphore()
    greeted = [(up_x, me_y), (down_x, me_y), (me_x, up_y), (me_x, down_y), (up_x, up_y), (down_x, down_y),
               (me_x, opposite), (me_x, cross)]
    for device in greeted:
        pl.semaphore_signal(barrier, inc=1, device_id=device, device_id_type=MESH)

    lane = lax.broadcasted_iota(jnp.int32, (CHUNK, cols), 1)
    first_lane = lane == 0
    last_lane = lane == cols - 1
    lane_full = lax.broadcasted_iota(jnp.int32, (rows, cols), 1)

    def describe(step, slot, source, target, device):
        return pltpu.make_async_remote_copy(
            src_ref=source, dst_ref=target, send_sem=send_sem.at[step, slot], recv_sem=recv_sem.at[step, slot],
            device_id=device, device_id_type=MESH)

    def send(step, slot, source, target, device):
        copy = describe(step, slot, source, target, device)
        copy.start()
        return copy

    def cross_send(step, c, source, device):
        return describe(step, 9 + c, source, near.at[step, 2, c], (me_x, device))

    def surface_sends(step, source):
        out = []
        for c in range(3):
            out.append(send(step, 6 + c, source.at[c], near.at[step, 0, c], (me_x, opposite)))

        @pl.when(direct)
        def _():
            for c in range(3):
                cross_send(step, c, source.at[c], cross).start()
        return out

    for c in range(3):
        ubuf[c, depth] = jnp.zeros((rows + 8, cols), F32)
    c1buf[rows:rows + 8] = jnp.zeros((8, cols), F32)
    c2buf[0:8] = jnp.zeros((8, cols), F32)
    c2buf[rows + 8:rows + 16] = jnp.zeros((8, cols), F32)
    mbuf[depth - 1] = jnp.zeros((rows, cols), F32)

    def halo_pack(step, layers, fresh):
        base = step * (rows + 8)
        packed = jnp.zeros((rows, cols), F32) if fresh else col_send[base:base + rows]
        for c in range(3):
            for k in layers:
                idx = c * depth + k
                row_send[step, idx:idx + 1] = ubuf[c, k, 0:1]
                value = ubuf[c, k, 0:rows]
                moved = value if idx == 0 else pltpu.roll(value, idx, 1)
                packed = jnp.where(lane_full == idx, moved, packed)
        col_send[base:base + rows] = packed

    def halo_sends(step):
        base = step * (rows + 8)
        return (send(step, 0, row_send.at[step], row_recv.at[step], (up_x, me_y)),
                send(step, 1, col_send.at[base:base + rows], col_recv.at[step, 0:rows], (me_x, up_y)),
                send(step, 2, col_send.at[base:base + 8], col_recv.at[step, rows:rows + 8], (up_x, up_y)))

    loads[0].wait()
    halo_pack(0, range(depth), True)
    pl.semaphore_wait(barrier, 8)
    halo = halo_sends(0)
    surface = surface_sends(0, u_in.at[:, 0])
    loads[1].wait()
    row_at = lax.broadcasted_iota(jnp.int32, (rows, cols), 0) + me_x * rows
    col_at = lane_full + me_y * cols
    valid = ((row_at < count_gx * rows - 1) & (col_at < count_gy * cols - 1)
             & (col_at != count_gy * cols // 2 + cols // 2 - 1))
    for k in range(depth - 1):
        mbuf[k] = jnp.where(valid, mbuf[k] * (1.0 / 16.0), 0.0)
    loads[2].wait()

    wide = 8 * rows
    raw = ibuf[0:wide]
    place = jnp.where(raw >= 0, raw, raw + DEAD)
    which = lax.rem(lax.broadcasted_iota(jnp.int32, (wide, cols), 0), 8)
    target = jnp.where(which < 6, which * (3 * rows) + place, -1)
    lane_wide = lax.broadcasted_iota(jnp.int32, (wide, cols), 1)
    for j in range(6 * 3 * rows // cols):
        onehot[:, j * cols:(j + 1) * cols] = jnp.where(lane_wide + j * cols == target, 1.0, 0.0).astype(BF16)
    raw_t = ibuf[wide:wide + 8][0:1]
    place_t = jnp.where(raw_t >= 0, raw_t, raw_t + DEAD)
    onehot_t[...] = jnp.where(
        lax.broadcasted_iota(jnp.int32, (3 * rows, cols), 0) == place_t, 1.0, 0.0).astype(BF16)
    live = ibuf[pl.ds(0, rows, stride=8)] >= 0

    for step in range(STEPS):
        for copy in halo:
            copy.wait()
        for c in range(3):
            for k in range(depth):
                ubuf[c, k, rows:rows + 1] = row_recv[step, c * depth + k:c * depth + k + 1]

        def chunk_body(chunk):
            r0 = chunk * CHUNK
            here = pl.ds(r0, CHUNK)
            below = pl.ds(r0 + 1, CHUNK)
            edge = col_recv[step, here]
            edge_below = col_recv[step, below]
            edge_sum = edge + edge_below
            edge_diff = edge_below - edge

            def shifted(value, side, idx):
                return jnp.where(last_lane, pltpu.roll(side, (cols - 1 - idx) % cols, 1), pltpu.roll(value, cols - 1, 1))

            def layer(k):
                out = []
                for c in range(3):
                    own = ubuf[c, k, here]
                    under = ubuf[c, k, below]
                    total = own + under
                    diff = under - own
                    idx = min(c * depth + k, 3 * depth - 1)
                    total_next = shifted(total, edge_sum, idx)
                    diff_next = shifted(diff, edge_diff, idx)
                    out.append((total + total_next, diff + diff_next, total_next - total))
                return out

            previous = layer(0)
            held = None
            pack1 = jnp.zeros((CHUNK, cols), F32)
            pack2 = jnp.zeros((CHUNK, cols), F32)
            for k in range(depth):
                if k < depth - 1:
                    current = layer(k + 1)
                    deform = [[current[c][0] - previous[c][0], previous[c][1] + current[c][1],
                               previous[c][2] + current[c][2]] for c in range(3)]
                    for c in range(3):
                        deform[c][c] = deform[c][c] + 4.0
                    previous = current
                    cofactor = [[deform[(c + 1) % 3][(d + 1) % 3] * deform[(c + 2) % 3][(d + 2) % 3]
                                 - deform[(c + 1) % 3][(d + 2) % 3] * deform[(c + 2) % 3][(d + 1) % 3]
                                 for d in range(3)] for c in range(3)]
                    jacobian = (deform[0][0] * cofactor[0][0] + deform[0][1] * cofactor[0][1]
                                + deform[0][2] * cofactor[0][2])
                    modulus = mbuf[k, here]
                    weight = modulus * (jacobian * (1.0 / 128.0) - 0.75)
                    quarter = [[modulus * deform[c][d] + weight * cofactor[c][d] for d in range(3)] for c in range(3)]
                for c in range(3):
                    if k == 0:
                        a, b, e = quarter[c]
                    elif k < depth - 1:
                        a = quarter[c][0] - held[c][0]
                        b = quarter[c][1] + held[c][1]
                        e = quarter[c][2] + held[c][2]
                    else:
                        a, b, e = -held[c][0], held[c][1], held[c][2]
                    plus = a + e
                    minus = a - e
                    z1 = minus + b
                    z2 = minus - b
                    idx = c * depth + k
                    f1buf[c, k, here] = (plus + b) + jnp.where(first_lane, 0.0, pltpu.roll(z1, 1, 1))
                    wbuf[c, k, pl.ds(r0 + 8, CHUNK)] = (plus - b) + jnp.where(first_lane, 0.0, pltpu.roll(z2, 1, 1))
                    pack1 = jnp.where(lane == idx, pltpu.roll(z1, idx + 1, 1), pack1)
                    pack2 = jnp.where(lane == idx, pltpu.roll(z2, idx + 1, 1), pack2)
                held = quarter
            c1buf[here] = pack1
            c2buf[pl.ds(r0 + 8, CHUNK)] = pack2

        relay = []

        def forward(c):
            surface[c].wait()
            relay.append(send(step, 12 + c, near.at[step, 0, c], near.at[step, 1, c], (me_x, partner)))

            @pl.when(relayed)
            def _():
                cross_send(step, c, near.at[step, 0, c], beside).start()

        chunks = rows // CHUNK
        for chunk in range(chunks):
            chunk_body(chunk)
            if chunks - 4 <= chunk < chunks - 1:
                forward(chunk - (chunks - 4))
        for c in range(3):
            for k in range(depth):
                idx = c * depth + k
                rim_row_send[step, idx:idx + 1] = wbuf[c, k, rows + 7:rows + 8]
        rim_col_send[step] = c1buf[0:rows + 8] + c2buf[7:rows + 15]
        rims = (send(step, 3, rim_row_send.at[step], rim_row_recv.at[step], (down_x, me_y)),
                send(step, 4, rim_col_send.at[step, 0:rows], rim_col_recv.at[step], (me_x, down_y)),
                send(step, 5, rim_col_send.at[step, rows:rows + 8], rim_diag_recv.at[step], (down_x, down_y)))

        def split_slot(slot):
            for c in range(3):
                value = near[step, slot, c]
                high = value.astype(BF16)
                low = (value - high.astype(F32)).astype(BF16)
                split[c * 3 * rows + slot * rows:c * 3 * rows + (slot + 1) * rows] = high
                split[(c + 3) * 3 * rows + slot * rows:(c + 3) * 3 * rows + (slot + 1) * rows] = low

        split_slot(0)
        for copy in relay:
            copy.wait()
        split_slot(1)
        for c in range(3):
            cross_send(step, c, near.at[step, 0, c], cross_way).wait()
        split_slot(2)
        gathered[...] = jnp.dot(onehot[...], split[...], preferred_element_type=F32).astype(BF16)
        if step == 0:
            for load in loads[4:7]:
                load.wait()

        group = 16

        def project(i, carry):
            for g in range(group):
                pair = i * group + g
                at16 = pl.multiple_of(pair * 16, 16)
                couple = mort[pl.ds(pl.multiple_of(pair * 2 * cols, 2 * cols), 2 * cols)]
                result = lax.dot_general(gathered[pl.ds(at16, 16)], couple, (((1,), (1,)), ((), ())),
                                         preferred_element_type=F32)
                projected[pl.ds(at16, 8)] = result[0:8, 0:cols]
                projected[pl.ds(at16 + 8, 8)] = result[8:16, cols:2 * cols]
            return carry

        lax.fori_loop(0, rows // 2 // group, project, 0)
        gap = gapbuf[...]
        for c in range(3):
            shadow = projected[pl.ds(c, rows, stride=8)] + projected[pl.ds(c + 3, rows, stride=8)]
            gap = gap + nbuf[c] * (ubuf[c, 0, 0:rows] - shadow)
        pressure = jnp.where(live, PENALTY * jnp.maximum(-gap, 0.0), 0.0)
        for c in range(3):
            force = pressure * nbuf[c]
            slave[c] = force
            high = force.astype(BF16).astype(F32)
            forces_lhs[pl.ds(c, rows, stride=8)] = high
            forces_lhs[pl.ds(c + 3, rows, stride=8)] = force - high
            if c < 2:
                forces_lhs[pl.ds(c + 6, rows, stride=8)] = jnp.zeros((rows, cols), F32)

        upper = lax.broadcasted_iota(jnp.int32, (16, cols), 0) < 8

        def react(i, carry):
            for g in range(group):
                pair = i * group + g
                at16 = pl.multiple_of(pair * 16, 16)
                couple = mort[pl.ds(pl.multiple_of(pair * 2 * cols, 2 * cols), 2 * cols)]
                both = forces_lhs[pl.ds(at16, 16)]
                left = jnp.concatenate([jnp.where(upper, both, 0.0), jnp.where(upper, 0.0, both)], 1).astype(BF16)
                reacted[pl.ds(at16, 16)] = jnp.dot(left, couple, preferred_element_type=F32)
            return carry

        lax.fori_loop(0, rows // 2 // group, react, 0)
        highs, lows = [], []
        for c in range(3):
            value = -(reacted[pl.ds(c, rows, stride=8)] + reacted[pl.ds(c + 3, rows, stride=8)])
            high = value.astype(BF16)
            highs.append(high)
            lows.append((value - high.astype(F32)).astype(BF16))
        stack = jnp.concatenate([jnp.concatenate(highs, 1), jnp.concatenate(lows, 1)], 0)
        scattered = jnp.dot(onehot_t[...], stack, preferred_element_type=F32)
        for slot in (1, 2, 0):
            for c in range(3):
                returned[step, slot, c] = scattered[slot * rows:(slot + 1) * rows, c * cols:(c + 1) * cols]
        back_partner = [send(step, 15 + c, returned.at[step, 1, c], relay_recv.at[step, c], (me_x, partner))
                        for c in range(3)]
        back_cross = [send(step, 18 + c, returned.at[step, 2, c], cross_recv.at[step, c], (me_x, cross_way))
                      for c in range(3)]
        back_opp = []
        for c in range(3):
            back_partner[c].wait()
            combined[step, c] = returned[step, 0, c] + relay_recv[step, c]

            @pl.when(relayed)
            def _():
                back_cross[c].wait()
                combined[step, c] = combined[step, c] + cross_recv[step, c]
            back_opp.append(send(step, 21 + c, combined.at[step, c], opp_recv.at[step, c], (me_x, opposite)))

        for copy in rims:
            copy.wait()
        if step == 0:
            loads[3].wait()
        corner = jnp.where(lax.broadcasted_iota(jnp.int32, (8, cols), 0) == 0, rim_diag_recv[step], 0.0)
        rim_col_recv[step, 0:8] = rim_col_recv[step, 0:8] + corner

        def update(k, extra):
            for c in range(3):
                idx = c * depth + k
                wbuf[c, k, 7:8] = rim_row_recv[step, idx:idx + 1]
                force = f1buf[c, k] + wbuf[c, k, 7:rows + 7]
                side = rim_col_recv[step]
                side = side if idx == 0 else pltpu.roll(side, cols - idx, 1)
                force = force + jnp.where(lane_full == 0, side, 0.0)
                if extra is not None:
                    force = force + extra[c]
                speed = DAMPING * vbuf[c, k] + TIME_STEP * force
                vbuf[c, k] = speed
                ubuf[c, k, 0:rows] = ubuf[c, k, 0:rows] + TIME_STEP * speed

        for k in range(1, depth):
            update(k, None)
        outs = []
        if step == STEPS - 1:
            outs = [pltpu.make_async_copy(vbuf.at[:, 1:depth], v_out.at[:, 1:depth], out_sem.at[0]),
                    pltpu.make_async_copy(ubuf.at[:, 1:depth, 0:rows], u_out.at[:, 1:depth], out_sem.at[1])]
            for copy in outs:
                copy.start()
        else:
            halo_pack(step + 1, range(1, depth), True)

        @pl.when(direct)
        def _():
            for copy in back_cross:
                copy.wait()
        for copy in back_opp:
            copy.wait()
        update(0, [slave[c] + opp_recv[step, c] + jnp.where(direct, cross_recv[step, c], 0.0) for c in range(3)])
        if step == STEPS - 1:
            last = [pltpu.make_async_copy(vbuf.at[:, 0], v_out.at[:, 0], out_sem.at[2]),
                    pltpu.make_async_copy(ubuf.at[:, 0, 0:rows], u_out.at[:, 0], out_sem.at[3])]
            for copy in last:
                copy.start()
            for copy in outs + last:
                copy.wait()
        else:
            halo_pack(step + 1, range(1), False)
            halo = halo_sends(step + 1)
            surface = surface_sends(step + 1, ubuf.at[:, 0, 0:rows])


def local(count_gx, count_gy, displacement, velocity, shear, normals, gap_zero, mortar, owner, blocks, live_rows):
    _, depth, rows, cols = displacement.shape
    column = lax.axis_index("gy")
    parity = lax.rem(column, 2)
    ahead = owner[:, 0] - lax.rem(column + count_gy // 2, count_gy) + 1
    ahead = jnp.where(ahead < 0, ahead + count_gy, jnp.where(ahead >= count_gy, ahead - count_gy, ahead))
    side = (ahead - 1) * (1 - 2 * parity)
    place = jnp.where(side < 0, 2, side) * rows + blocks[:, 0]
    place = jnp.where(jnp.arange(rows, dtype=jnp.int32) < live_rows[0, 0], place, place - DEAD)
    index = jnp.concatenate([jnp.broadcast_to(jnp.repeat(place, 8)[:, None], (8 * rows, cols)),
                             jnp.broadcast_to(jnp.tile(place, cols // rows)[None], (8, cols))], 0)
    any_space = pl.BlockSpec(memory_space=pl.ANY)
    vmem = pltpu.VMEM
    two = STEPS
    lines = 3 * depth
    scratch = [
        vmem((3, depth + 1, rows + 8, cols), F32), vmem((3, depth, rows, cols), F32), vmem((depth, rows, cols), F32),
        vmem((3, rows, cols), F32), vmem((rows, cols), F32), vmem((rows * cols, cols), BF16),
        vmem((8 * rows + 8, cols), jnp.int32),
        vmem((3, depth, rows, cols), F32), vmem((3, depth, rows + 8, cols), F32), vmem((rows + 8, cols), F32),
        vmem((rows + 16, cols), F32),
        vmem((two, lines, cols), F32), vmem((two, lines, cols), F32), vmem((two * (rows + 8), cols), F32),
        vmem((two, rows + 8, cols), F32),
        vmem((two, lines, cols), F32), vmem((two, lines, cols), F32), vmem((two, rows + 8, cols), F32),
        vmem((two, rows, cols), F32), vmem((two, 8, cols), F32),
        vmem((two, 3, 3, rows, cols), F32), vmem((18 * rows, cols), BF16), vmem((8 * rows, 18 * rows), BF16),
        vmem((3 * rows, cols), BF16), vmem((8 * rows, cols), BF16), vmem((8 * rows, cols), F32),
        vmem((8 * rows, cols), F32), vmem((8 * rows, cols), F32), vmem((two, 3, 3, rows, cols), F32),
        vmem((two, 3, rows, cols), F32), vmem((two, 3, rows, cols), F32),
        vmem((two, 3, rows, cols), F32), vmem((two, 3, rows, cols), F32), vmem((3, rows, cols), F32),
        pltpu.SemaphoreType.DMA((7,)), pltpu.SemaphoreType.DMA((4,)),
        pltpu.SemaphoreType.DMA((two, 24)), pltpu.SemaphoreType.DMA((two, 24)),
    ]
    return pl.pallas_call(
        functools.partial(kernel, count_gx, count_gy),
        out_shape=(jax.ShapeDtypeStruct(displacement.shape, F32), jax.ShapeDtypeStruct(velocity.shape, F32)),
        in_specs=[pl.BlockSpec(memory_space=pltpu.HBM)] * 7,
        out_specs=(any_space, any_space),
        scratch_shapes=scratch,
        compiler_params=pltpu.CompilerParams(collective_id=0, has_side_effects=True, vmem_limit_bytes=48 << 20),
    )(*[pltpu.with_memory_space_constraint(x, pltpu.HBM) for x in (displacement, velocity, shear, normals, gap_zero, mortar.reshape(rows * cols, cols))], index)


def solution(mesh):
    in_specs = (
        P(None, None, "gx", "gy"),
        P(None, None, "gx", "gy"),
        P(None, "gx", "gy"),
        P(None, "gx", "gy"),
        P("gx", "gy"),
        P("gx", "gy", None, None),
        P("gx", "gy"),
        P("gx", "gy"),
        P("gx", "gy"),
    )
    out_specs = (P(None, None, "gx", "gy"), P(None, None, "gx", "gy"))
    step = functools.partial(local, mesh.shape["gx"], mesh.shape["gy"])
    return jax.shard_map(step, mesh=mesh, in_specs=in_specs, out_specs=out_specs, check_vma=False)
```
